512 devices in a mesh: pipe: 32 (over z_hi, y), dp: 16 (over x, z_lo, core).
Axes of the slice: x: 4, y: 8, z: 8 (z_hi: 4, z_lo: 2; z = z_hi * 2 + z_lo), core: 2. Of those that a mesh axis runs over, the one named last changes fastest.
Arguments:
- section_inputs: bfloat16 [32, 3072, 6144], P('pipe', 'dp'), may hold values from -6 to 6
- loss_grad: bfloat16 [3072, 6144], P('dp', 'pipe'), may hold values from -6 to 6
- weight_blocks: bfloat16 [32, 48, 128, 128], P('pipe', 'dp'), may hold values from -0.3125 to 0.3125
- left_factor: bfloat16 [32, 6144, 64], P('pipe', 'dp'), may hold values from -0.078125 to 0.078125
- right_factor: bfloat16 [32, 64, 6144], P('pipe', None, 'dp'), may hold values from -0.5 to 0.5
- block_column: int32 [32, 48], P('pipe'), may hold values from 0 to 47, each once within a row
- live_length: int32 [16, 12], P('dp'), may hold values from 1 to 16, 144 in all within a row
Outputs:
- in_grad: bfloat16 [32, 3072, 6144], P('pipe', 'dp')
- grad_blocks: bfloat16 [32, 48, 128, 128], P('pipe', 'dp')
- grad_left: bfloat16 [32, 6144, 64], P('pipe', 'dp')
- grad_right: bfloat16 [32, 64, 6144], P('pipe', None, 'dp')
The draws below stay inside these ranges and needn't reach their ends.
Inputs may be any that keep to these rules, and one draw needn't show every extreme that they name: `block_column`: each section's row is a permutation of 0 to 47. `live_length`: each row sums to 144 live tokens.
All inputs are finite; a program needn't handle non-finite values.
Results may differ from the reference program's by a relative error of at most 0.035.
Values may be sent and summed in bfloat16 or wider, within the bound.
A program may use at most 64 MiB of HBM per device.

```python
import math
import jax
import jax.numpy as jnp
import numpy as np
from jax import lax

D = 6144
BLK = 128
RANK = 64
MB = 12
ROWS_MB = 16
NBR = 48
TOKENS = 3072
N_PIPE = 32
N_DP = 16


def with_spikes(array, key, source, target, blocks, factor):
    owner, partner = [(jnp.arange(array.shape[position]) // (array.shape[position] // blocks)).reshape([-1 if axis == position else 1 for axis in range(array.ndim)]) for position in (source, target)]
    chosen = jax.random.permutation(key, blocks)[partner]
    strong = (owner == chosen) | (owner == (partner + blocks // 2) % blocks)
    return jnp.where(strong, factor * array, array)


def levels(key, shape, split, low, high):
    factor_of = 1.0
    for axis_at, blocks in split:
        draws = jax.random.uniform(jax.random.fold_in(jax.random.fold_in(key, 6), axis_at), (blocks,), jnp.float32, low / len(split), high / len(split))
        factor_of = factor_of * jnp.repeat(jnp.exp(draws), shape[axis_at] // blocks).reshape((-1,) + (1,) * (len(shape) - 1 - axis_at))
    return factor_of


def profile(amount, total, most, lean):
    weights = [(1 << 20) // math.isqrt(standing ** lean) + 1 for standing in range(2, amount + 1)]
    surplus, given = total - most - (amount - 1), [1] * (amount - 1)
    while surplus > 0:
        free = [i for i in range(amount - 1) if given[i] < most]
        whole, remaining = sum([weights[i] for i in free]), surplus
        for i in free:
            addition = min(most - given[i], max(1, remaining * weights[i] // whole), surplus)
            given[i] = given[i] + addition
            surplus = surplus - addition
    return np.array([most] + given)


def uneven_parts(rng, amount, total, reach, lean):
    if amount == 2:
        one = jax.random.randint(rng, (), max(1, total - reach), min(reach, total - 1) + 1)
        return jnp.stack([one, total - one])
    lengths = jnp.asarray(profile(amount, total, reach, lean), jnp.int32)
    pairs = (amount - 1) // 2
    source_of, taker = lengths[1:1 + 2 * pairs:2], lengths[2:2 + 2 * pairs:2]
    slack = jnp.minimum(source_of - 1, reach - taker)
    shifted = jax.random.randint(jax.random.fold_in(rng, 1), (pairs,), 0, 1 << 20) % (slack + 1)
    lengths = lengths.at[1:1 + 2 * pairs:2].set(source_of - shifted).at[2:2 + 2 * pairs:2].set(taker + shifted)
    return lengths[jax.random.permutation(jax.random.fold_in(rng, 2), amount)]


def centred(own_key, extent, spread, most, pieces=(), kind=jnp.bfloat16):
    result = jax.random.normal(own_key, extent, jnp.float32) * spread
    if len(pieces) > 0:
        result = levels(own_key, extent, pieces, -0.22, 0.18) * result
    return jnp.clip(result, min=-most, max=most).astype(kind)


def gaussian_with(own_key, extent, deviation, limit, cuts, heavy, held_as=jnp.bfloat16):
    entries = deviation * jax.random.normal(own_key, extent, jnp.float32)
    if cuts:
        entries = entries * levels(own_key, extent, cuts, -0.22, 0.18)
    return jnp.clip(with_spikes(entries, jax.random.fold_in(own_key, 3), *heavy), -limit, limit).astype(held_as)


def setup_inputs(seed: int = 0) -> dict:
    keys = jax.random.split(jax.random.key(seed), 8)
    section_inputs = gaussian_with(keys[0], (N_PIPE, TOKENS, D), 1.0, 6.0, ((0, 32), (1, 16)), (1, 2, 16, 2.0))
    loss_grad = centred(keys[1], (TOKENS, D), 1.0, 6.0, ((0, 16), (1, 32)))
    weight_blocks = centred(keys[2], (N_PIPE, NBR, BLK, BLK), (0.25 / BLK ** 0.5), 0.3125, ((0, 32), (1, 16)))
    left_factor = centred(keys[3], (N_PIPE, D, RANK), D ** -0.5, 0.078125, ((0, 32), (1, 16)))
    right_factor = centred(keys[4], (N_PIPE, RANK, D), (0.25 / RANK ** 0.5), 0.5, ((0, 32), (2, 16)))
    block_column = jax.vmap(lambda own: jax.random.permutation(own, NBR))(jax.random.split(keys[5], N_PIPE)).reshape((N_PIPE, NBR)).astype(jnp.int32)
    live_length = jax.vmap(lambda own: uneven_parts(own, MB, MB * ROWS_MB * 3 // 4, ROWS_MB, 1))(jax.random.split(keys[6], N_DP)).reshape((N_DP, MB)).astype(jnp.int32)
    return {"section_inputs": section_inputs, "loss_grad": loss_grad, "weight_blocks": weight_blocks, "left_factor": left_factor, "right_factor": right_factor, "block_column": block_column, "live_length": live_length}


def slope_of(values):
    cumulative = 0.5 * (1.0 + jax.scipy.special.erf(values * (1.0 / math.sqrt(2.0))))
    density = jnp.exp(-0.5 * values * values) * (1.0 / math.sqrt(2.0 * math.pi))
    return cumulative + values * density

def inverse_of(columns):
    number = columns.shape[0]
    ladder = jnp.arange(number, dtype=jnp.int32)
    matches = (columns[:, None] == ladder[None, :]).astype(jnp.int32)
    return lax.optimization_barrier(jnp.sum(matches * ladder[:, None], axis=0)).astype(jnp.int32)

def section_pass(inputs, incoming, blocks, left_factor, right_factor, columns):
    row_count, features = inputs.shape
    number, block_size = (blocks.shape[0], blocks.shape[1])
    inverse = inverse_of(columns)
    split_in = inputs.astype(jnp.float32).reshape(row_count, number, block_size)
    wide_blocks = blocks.astype(jnp.float32)
    sparse = jnp.einsum('tnb,nbc->tnc', split_in, wide_blocks)
    sparse = jnp.take(sparse, inverse, axis=1).reshape(row_count, features)
    lowered = jnp.dot(inputs, left_factor, preferred_element_type=jnp.float32).astype(jnp.bfloat16)
    preactivation = sparse + jnp.dot(lowered, right_factor, preferred_element_type=jnp.float32)
    delta_grad = (incoming.astype(jnp.float32) * slope_of(preactivation)).astype(jnp.bfloat16)
    delta_split = jnp.take(delta_grad.reshape(row_count, number, block_size), columns, axis=1)
    back_sparse = jnp.einsum('tnc,nbc->tnb', delta_split.astype(jnp.float32), wide_blocks).reshape(row_count, features)
    reduced = jnp.einsum('td,rd->tr', delta_grad.astype(jnp.float32), right_factor.astype(jnp.float32)).astype(jnp.bfloat16)
    back_low = jnp.einsum('tr,dr->td', reduced.astype(jnp.float32), left_factor.astype(jnp.float32))
    outgoing = (incoming.astype(jnp.float32) + back_sparse + back_low).astype(jnp.bfloat16)
    return (outgoing, delta_grad, delta_split, lowered, reduced)

def total_of(partial_value):
    rounded = lax.optimization_barrier(partial_value.astype(jnp.bfloat16))
    return lax.optimization_barrier(jnp.sum(rounded.astype(jnp.float32), axis=0)).astype(jnp.bfloat16)

def group_terms(inputs, delta_grad, delta_split, lowered, reduced, number, block_size):
    groups = N_DP
    wide_in = inputs.astype(jnp.float32).reshape(groups, -1, D)
    split_in = wide_in.reshape(groups, -1, number, block_size)
    split_delta = delta_split.astype(jnp.float32).reshape(groups, -1, number, block_size)
    part_blocks = jnp.einsum('gtnb,gtnc->gnbc', split_in, split_delta)
    part_left = jnp.einsum('gtd,gtr->gdr', wide_in, reduced.astype(jnp.float32).reshape(groups, -1, RANK))
    part_right = jnp.einsum('gtr,gtd->grd', lowered.astype(jnp.float32).reshape(groups, -1, RANK), delta_grad.astype(jnp.float32).reshape(groups, -1, D))
    return (total_of(part_blocks), total_of(part_left), total_of(part_right))

def reference(section_inputs, loss_grad, weight_blocks, left_factor, right_factor, block_column, live_length):
    positions = jnp.arange(TOKENS, dtype=jnp.int32)
    limits = jnp.take(live_length.reshape(-1), (positions // ROWS_MB).astype(jnp.int32))
    live = positions % ROWS_MB < limits
    seeded = jnp.where(live[:, None], loss_grad, jnp.zeros_like(loss_grad))

    def one_section(incoming, slices):
        inputs, blocks, left_one, right_one, columns = slices
        outgoing, delta_grad, delta_split, lowered, reduced = section_pass(inputs, incoming, blocks, left_one, right_one, columns)
        grads = group_terms(inputs, delta_grad, delta_split, lowered, reduced, blocks.shape[0], blocks.shape[1])
        return (outgoing, (outgoing, grads[0], grads[1], grads[2]))
    unused, stacked = lax.scan(one_section, seeded, (section_inputs, weight_blocks, left_factor, right_factor, block_column), reverse=True)
    return (stacked[0], stacked[1], stacked[2], stacked[3])
```

```python
import functools
import math

import jax
import jax.numpy as jnp
from jax import lax
from jax.experimental import pallas as pl
from jax.experimental.pallas import tpu as pltpu
from jax.sharding import PartitionSpec as P

MESH = pl.DeviceIdType.MESH
LIVE = 144
ROWS = 16
CHUNKS = 4
VMEM = pl.BlockSpec(memory_space=pltpu.VMEM)
SMEM = pl.BlockSpec(memory_space=pltpu.SMEM)
LIMIT = 60 * 1024 * 1024


def slope_of(values):
    cumulative = 0.5 * (1.0 + jax.scipy.special.erf(values * (1.0 / math.sqrt(2.0))))
    density = jnp.exp(-0.5 * values * values) * (1.0 / math.sqrt(2.0 * math.pi))
    return cumulative + values * density


def inverse_of(columns):
    number = columns.shape[0]
    ladder = jnp.arange(number, dtype=jnp.int32)
    matches = (columns[:, None] == ladder[None, :]).astype(jnp.int32)
    return jnp.sum(matches * ladder[:, None], axis=0)


def greet_group(count, me):
    barrier = pltpu.get_barrier_semaphore()
    for by in range(1, count):
        pl.semaphore_signal(
            barrier, inc=1, device_id={"dp": lax.rem(me + by, count)}, device_id_type=MESH
        )
    pl.semaphore_wait(barrier, count - 1)


def gather_kernel(count, own_ref, whole_ref, send_sem, recv_sem, local_sem):
    me = lax.axis_index("dp")
    greet_group(count, me)
    copies = []
    for by in range(1, count):
        copy = pltpu.make_async_remote_copy(
            src_ref=own_ref,
            dst_ref=whole_ref.at[me],
            send_sem=send_sem.at[by],
            recv_sem=recv_sem.at[by],
            device_id={"dp": lax.rem(me + by, count)},
            device_id_type=MESH,
        )
        copy.start()
        copies.append(copy)
    local = pltpu.make_async_copy(own_ref, whole_ref.at[me], local_sem)
    local.start()
    local.wait()
    for copy in copies:
        copy.wait()


def gather_dp(own, count):
    return pl.pallas_call(
        functools.partial(gather_kernel, count),
        out_shape=jax.ShapeDtypeStruct((count,) + own.shape, own.dtype),
        in_specs=[VMEM],
        out_specs=VMEM,
        scratch_shapes=[
            pltpu.SemaphoreType.DMA((count,)),
            pltpu.SemaphoreType.DMA((count,)),
            pltpu.SemaphoreType.DMA,
        ],
        compiler_params=pltpu.CompilerParams(
            collective_id=0, has_side_effects=True, vmem_limit_bytes=LIMIT
        ),
    )(own)


def reduce_kernel(count, parts_ref, sum_ref, landed, send_sem, recv_sem, local_sem):
    me = lax.axis_index("dp")
    greet_group(count, me)
    copies = []
    for by in range(1, count):
        target = lax.rem(me + by, count)
        copy = pltpu.make_async_remote_copy(
            src_ref=parts_ref.at[target],
            dst_ref=landed.at[by],
            send_sem=send_sem.at[by],
            recv_sem=recv_sem.at[by],
            device_id={"dp": target},
            device_id_type=MESH,
        )
        copy.start()
        copies.append(copy)
    local = pltpu.make_async_copy(parts_ref.at[me], landed.at[0], local_sem)
    local.start()
    local.wait()
    for copy in copies:
        copy.wait()
    height = 64

    def some_rows(at, carry):
        rows = pl.ds(at * height, height)
        total = jnp.sum(landed[:, rows, :].astype(jnp.float32), axis=0)
        sum_ref[rows, :] = total.astype(sum_ref.dtype)
        return carry

    lax.fori_loop(0, sum_ref.shape[0] // height, some_rows, 0)


def reduce_dp(parts):
    count = parts.shape[0]
    return pl.pallas_call(
        functools.partial(reduce_kernel, count),
        out_shape=jax.ShapeDtypeStruct(parts.shape[1:], parts.dtype),
        in_specs=[VMEM],
        out_specs=VMEM,
        scratch_shapes=[
            pltpu.VMEM(parts.shape, parts.dtype),
            pltpu.SemaphoreType.DMA((count,)),
            pltpu.SemaphoreType.DMA((count,)),
            pltpu.SemaphoreType.DMA,
        ],
        compiler_params=pltpu.CompilerParams(
            collective_id=1, has_side_effects=True, vmem_limit_bytes=LIMIT
        ),
    )(parts)


def pipe_kernel(
    sections,
    cols_ref,
    head_ref,
    slope_ref,
    mats_ref,
    left_ref,
    out_ref,
    delta_ref,
    red_ref,
    g_ref,
    back_ref,
    send_sem,
    recv_sem,
):
    section = lax.axis_index("pipe")
    last = sections - 1
    after = lax.rem(section + sections - 1, sections)
    steps, number, rows, width = g_ref.shape
    rank = left_ref.shape[0]
    span = number // CHUNKS
    barrier = pltpu.get_barrier_semaphore()

    for neighbour in (after, lax.rem(section + 1, sections)):
        pl.semaphore_signal(barrier, inc=1, device_id={"pipe": neighbour}, device_id_type=MESH)
    pl.semaphore_wait(barrier, 2)

    def hop(step, chunk):
        part = pl.ds(chunk * span, span)
        return pltpu.make_async_remote_copy(
            src_ref=out_ref.at[step, part],
            dst_ref=g_ref.at[step, part],
            send_sem=send_sem.at[step * CHUNKS + chunk],
            recv_sem=recv_sem.at[step * CHUNKS + chunk],
            device_id={"pipe": after},
            device_id_type=MESH,
        )

    def one_step(step, carry):
        here = pl.ds(pl.multiple_of(step * rows, rows), rows)
        total = jnp.zeros((rows, rank), jnp.float32)
        for chunk in range(CHUNKS):
            part = pl.ds(chunk * span, span)

            @pl.when(section == last)
            def _():
                g_ref[step, part] = head_ref[step, part]

            @pl.when(section < last)
            def _():
                hop(step, chunk).wait_recv()

            delta = g_ref[step, part].astype(jnp.float32) * slope_ref[part, here, :]
            delta = delta.astype(jnp.bfloat16)
            delta_ref[part, here, :] = delta
            both = lax.dot_general(
                delta,
                mats_ref[part],
                (((2,), (1,)), ((0,), (0,))),
                preferred_element_type=jnp.float32,
            )
            back_ref[part] = both[:, :, :width]
            total = total + jnp.sum(both[:, :, width:], axis=0)
        reduced = total.astype(jnp.bfloat16)
        red_ref[here, :] = reduced
        for chunk in range(CHUNKS):
            low = jnp.dot(
                reduced,
                left_ref[:, chunk * span * width : (chunk + 1) * span * width],
                preferred_element_type=jnp.float32,
            )
            for at in range(span):
                block = chunk * span + at
                fresh = g_ref[step, block].astype(jnp.float32) + back_ref[cols_ref[block]]
                fresh = fresh + low[:, at * width : (at + 1) * width]
                out_ref[step, block] = fresh.astype(jnp.bfloat16)

            @pl.when(section > 0)
            def _():
                hop(step, chunk).start()

        return carry

    lax.fori_loop(0, steps, one_step, 0)

    @pl.when(section > 0)
    def _():
        def drain(step, carry):
            for chunk in range(CHUNKS):
                hop(step, chunk).wait_send()
            return carry

        lax.fori_loop(0, steps, drain, 0)


def run_pipe(sections, columns, head, slope, mats, left_turned):
    steps, number, rows, width = head.shape
    rank = left_turned.shape[0]
    return pl.pallas_call(
        functools.partial(pipe_kernel, sections),
        out_shape=(
            jax.ShapeDtypeStruct(head.shape, jnp.bfloat16),
            jax.ShapeDtypeStruct((number, steps * rows, width), jnp.bfloat16),
            jax.ShapeDtypeStruct((steps * rows, rank), jnp.bfloat16),
        ),
        in_specs=[SMEM, VMEM, VMEM, VMEM, VMEM],
        out_specs=(VMEM, VMEM, VMEM),
        scratch_shapes=[
            pltpu.VMEM(head.shape, jnp.bfloat16),
            pltpu.VMEM((number, rows, width), jnp.float32),
            pltpu.SemaphoreType.DMA((steps * CHUNKS,)),
            pltpu.SemaphoreType.DMA((steps * CHUNKS,)),
        ],
        compiler_params=pltpu.CompilerParams(
            collective_id=2, has_side_effects=True, vmem_limit_bytes=LIMIT
        ),
    )(columns, head, slope, mats, left_turned)


def body(
    section_inputs, loss_grad, weight_blocks, left_factor, right_factor, block_column, live_length
):
    inputs = section_inputs[0]
    columns = block_column[0]
    inverse = inverse_of(columns)
    sections = lax.axis_size("pipe")
    group = lax.axis_size("dp")
    tokens, features = inputs.shape
    micro_count = live_length.shape[1]
    micro_rows = tokens // micro_count
    own_blocks, width = weight_blocks.shape[1], weight_blocks.shape[2]
    number = own_blocks * group
    rank = left_factor.shape[2]
    steps = LIVE // ROWS

    own = jnp.concatenate(
        [
            weight_blocks[0].reshape(own_blocks * width, width),
            jnp.concatenate([left_factor[0], right_factor[0].T], axis=1),
        ],
        axis=0,
    )
    whole = gather_dp(own, group)
    blocks = whole[:, : own_blocks * width].reshape(number, width, width)
    left = whole[:, own_blocks * width :, :rank].reshape(features, rank)
    right_turned = whole[:, own_blocks * width :, rank:].reshape(number, width, rank)
    blocks_at = jnp.take(blocks, inverse, axis=0)
    mats = jnp.concatenate([jnp.swapaxes(blocks_at, 1, 2), right_turned], axis=2)

    lengths = live_length[0]
    micro = jnp.arange(micro_count, dtype=jnp.int32)
    starts = jnp.sum(jnp.where(micro[None, :] < micro[:, None], lengths[None, :], 0), axis=1)
    inside = jnp.arange(micro_rows, dtype=jnp.int32)
    place = jnp.where(inside[None, :] < lengths[:, None], starts[:, None] + inside[None, :], LIVE)
    place = place.reshape(tokens)
    chosen = (jnp.arange(LIVE, dtype=jnp.int32)[:, None] == place[None, :]).astype(jnp.bfloat16)

    seeds = jnp.dot(chosen, loss_grad, preferred_element_type=jnp.float32).astype(jnp.bfloat16)
    head = lax.all_gather(seeds, "pipe", axis=1, tiled=True)
    head = jnp.swapaxes(head.reshape(steps, ROWS, number, width), 1, 2)

    live = jnp.dot(chosen, inputs, preferred_element_type=jnp.float32).astype(jnp.bfloat16)
    live_blocks = jnp.swapaxes(live.reshape(LIVE, number, width), 0, 1)
    live_at = jnp.take(live_blocks, inverse, axis=0)
    lowered = jnp.dot(live, left, preferred_element_type=jnp.float32).astype(jnp.bfloat16)
    before = jnp.einsum("jtb,jbc->jtc", live_at, blocks_at, preferred_element_type=jnp.float32)
    before = before + jnp.einsum(
        "tr,jcr->jtc", lowered, right_turned, preferred_element_type=jnp.float32
    )
    slope = slope_of(before)

    outgoing, delta, reduced = run_pipe(sections, columns, head, slope, mats, left.T)

    flat = jnp.swapaxes(outgoing, 1, 2).reshape(LIVE, features)
    in_grad = lax.dot_general(
        chosen, flat, (((0,), (0,)), ((), ())), preferred_element_type=jnp.float32
    ).astype(jnp.bfloat16)

    grad_at = jnp.einsum("jtb,jtc->jbc", live_at, delta, preferred_element_type=jnp.float32)
    grad_blocks = jnp.take(grad_at.astype(jnp.bfloat16), columns, axis=0)
    grad_left = jnp.einsum("td,tr->dr", live, reduced, preferred_element_type=jnp.float32)
    grad_right = jnp.einsum("jtc,tr->jcr", delta, lowered, preferred_element_type=jnp.float32)
    factors = jnp.concatenate([grad_left, grad_right.reshape(features, rank)], axis=1)
    parts = jnp.concatenate(
        [
            grad_blocks.reshape(group, own_blocks * width, width),
            factors.astype(jnp.bfloat16).reshape(group, features // group, 2 * rank),
        ],
        axis=1,
    )
    sums = reduce_dp(parts)
    sum_factors = sums[own_blocks * width :]
    return (
        in_grad[None],
        sums[: own_blocks * width].reshape(1, own_blocks, width, width),
        sum_factors[None, :, :rank],
        sum_factors[:, rank:].T[None],
    )


def solution(mesh):
    in_specs = (
        P("pipe", "dp", None),
        P("dp", "pipe"),
        P("pipe", "dp", None, None),
        P("pipe", "dp", None),
        P("pipe", None, "dp"),
        P("pipe", None),
        P("dp", None),
    )
    out_specs = (
        P("pipe", "dp", None),
        P("pipe", "dp", None, None),
        P("pipe", "dp", None),
        P("pipe", None, "dp"),
    )
    return jax.shard_map(body, mesh=mesh, in_specs=in_specs, out_specs=out_specs, check_vma=False)
```
